32 devices in a mesh: groups: 2 (over x), seq: 16 (over z, y, core).
Axes of the slice: x: 2, y: 2, z: 4, core: 2. Of those that a mesh axis runs over, the one named last changes fastest.
Arguments:
- query_vals: bfloat16 [24576, 2048], P(('groups', 'seq')), parts along dimension 0, may hold values from -6 to 6
- query_scale: float32 [192, 16], P(('groups', 'seq')), parts along dimension 0, may hold values from 0.6 to 1.6
- key_vals: bfloat16 [24576, 2048], P(('groups', 'seq')), parts along dimension 0, may hold values from -8 to 8
- key_scale: float32 [192, 16], P(('groups', 'seq')), parts along dimension 0, may hold values from 0.6 to 1.6
- value_vals: bfloat16 [24576, 2048], P(('groups', 'seq')), parts along dimension 0, may hold values from -8 to 8
- value_scale: float32 [192, 16], P(('groups', 'seq')), parts along dimension 0, may hold values from 0.6 to 1.6
- feature_matrix: bfloat16 [128, 256], replicated, may hold values from -5 to 5
- cotangent: bfloat16 [24576, 2048], P(('groups', 'seq')), parts along dimension 0, may hold values from -6 to 6
Outputs:
- attended: bfloat16 [24576, 2048], P(('groups', 'seq')), parts along dimension 0
- query_grad: bfloat16 [24576, 2048], P(('groups', 'seq')), parts along dimension 0
- key_grad: bfloat16 [24576, 2048], P(('groups', 'seq')), parts along dimension 0
- value_grad: bfloat16 [24576, 2048], P(('groups', 'seq')), parts along dimension 0
The draws below stay inside these ranges and needn't reach their ends.
There are 2 independent parts, one for each index of `groups`. The reference program is written for one: setup_inputs(seed, part) draws one part's arguments, and reference() takes and returns one part's arrays. A program takes and returns all parts, laid end to end along the dimension named above; an argument that names none is the same for every part. Nothing has to cross between parts.
All inputs are finite; a program needn't handle non-finite values.
Results may differ from the reference program's by a relative error of at most 0.025.
Values sent between devices are 32-bit elements; how exact they have to be, the bound alone decides.
A program may use at most 128 MiB of HBM per device.

```python
import math
import jax
import jax.numpy as jnp
from jax import lax

H = 16
DH = 128
M = 256
BLK = 128
TOKENS = 12288


def block_field(key, mean_factor):
    blocks = TOKENS // BLK
    first_key, second_key = jax.random.split(key)
    means = jax.random.normal(first_key, (blocks, 1, H * DH), jnp.float32)
    noise = jax.random.normal(second_key, (blocks, BLK, H * DH), jnp.float32)
    field = mean_factor * means + noise
    return jnp.clip(field, -8.0, 8.0).reshape(TOKENS, H * DH).astype(jnp.bfloat16)


def draw_key_vals(key, part):
    return block_field(jax.random.fold_in(key, 11), 1.5)


def draw_value_vals(key, part):
    return block_field(jax.random.fold_in(key, 23), 1.0)


def block_scale(key, shape, shards, smallest, top_value):
    def one(axis_at, shards_of):
        steps = jax.random.uniform(jax.random.fold_in(jax.random.fold_in(key, 6), axis_at), (shards_of,), jnp.float32, smallest / len(shards), top_value / len(shards))
        return jnp.repeat(jnp.exp(steps), shape[axis_at] // shards_of).reshape((-1,) + (1,) * (len(shape) - axis_at - 1))

    gain = one(*shards[0])
    for cut in shards[1:]:
        gain = gain * one(*cut)
    return gain


def normal_values(own_key, dims, deviation, reach, shards=(), kind=jnp.bfloat16):
    gain = block_scale(own_key, dims, shards, -0.22, 0.18) if shards else 1.0
    entries = jax.random.normal(own_key, dims, jnp.float32) * deviation * gain
    return jnp.minimum(jnp.maximum(entries, -reach), reach).astype(kind)


def setup_inputs(seed: int = 0, part: int = 0) -> dict:
    key_list = jax.random.split(jax.random.key(seed), 9)
    part_splits = jax.random.split(jax.random.fold_in(key_list[8], part), 9)
    query_vals = normal_values(part_splits[0], (TOKENS, H * DH), 1.0, 6.0, ((0, 16),))
    query_scale = jnp.clip(jnp.exp(math.log(1.6) - 0.98082923 * jax.random.uniform(part_splits[1], (TOKENS // BLK, H), jnp.float32) ** block_scale(part_splits[1], (TOKENS // BLK, H), ((0, 16),), -0.2, 0.2)), 0.6, 1.6)
    key_vals = draw_key_vals(jax.random.fold_in(jax.random.fold_in(key_list[8], part), 71), part)
    key_scale = jnp.clip(jnp.exp(math.log(1.6) - 0.98082923 * jax.random.uniform(part_splits[3], (TOKENS // BLK, H), jnp.float32) ** block_scale(part_splits[3], (TOKENS // BLK, H), ((0, 16),), -0.2, 0.2)), 0.6, 1.6)
    value_vals = draw_value_vals(jax.random.fold_in(jax.random.fold_in(key_list[8], part), 71), part)
    value_scale = jnp.clip(jnp.exp(math.log(1.6) - 0.98082923 * jax.random.uniform(part_splits[5], (TOKENS // BLK, H), jnp.float32) ** block_scale(part_splits[5], (TOKENS // BLK, H), ((0, 16),), -0.2, 0.2)), 0.6, 1.6)
    feature_matrix = normal_values(key_list[6], (DH, M), 1.0, 5.0)
    cotangent = normal_values(part_splits[7], (TOKENS, H * DH), 1.0, 6.0, ((0, 16),))
    return dict(query_vals=query_vals, query_scale=query_scale, key_vals=key_vals, key_scale=key_scale, value_vals=value_vals, value_scale=value_scale, feature_matrix=feature_matrix, cotangent=cotangent)


def spread_scale(scale, count):
    blocks = scale.shape[0]
    return jnp.broadcast_to(scale[:, None, :], (blocks, count // blocks, scale.shape[1])).reshape(count, scale.shape[1])


def reference(query_vals, query_scale, key_vals, key_scale, value_vals, value_scale, feature_matrix, cotangent):
    count = query_vals.shape[0]
    root_four = DH ** 0.25
    root_two = DH ** 0.5

    def heads_first(values):
        return values.reshape(count, H, DH).transpose(1, 0, 2)

    def head_pass(operands):
        query_rows, query_factor, key_rows, key_factor, value_rows, value_factor, upstream = operands
        query_proj = jnp.dot(query_rows, feature_matrix, preferred_element_type=jnp.float32) * (query_factor / root_four)[:, None]
        query_random_features = jnp.exp(query_proj).astype(jnp.bfloat16)
        key_float = key_rows.astype(jnp.float32) * key_factor[:, None]
        key_proj = jnp.dot(key_rows, feature_matrix, preferred_element_type=jnp.float32) * (key_factor / root_four)[:, None]
        key_proj = key_proj - (jnp.sum(key_float * key_float, axis=1) / (2.0 * root_two))[:, None]
        key_random_features = jnp.exp(key_proj).astype(jnp.bfloat16)
        block_value = (value_rows.astype(jnp.float32) * value_factor[:, None]).astype(jnp.bfloat16)
        state = jnp.dot(key_random_features.T, block_value, preferred_element_type=jnp.float32)
        normalizer = jnp.sum(key_random_features.astype(jnp.float32), axis=0)
        total = jnp.sum(normalizer)
        block_state = (state / total).astype(jnp.bfloat16)
        query_float = query_random_features.astype(jnp.float32)
        attention_numerator = jnp.dot(query_random_features, block_state, preferred_element_type=jnp.float32)
        denominator = jnp.dot(query_float, normalizer, precision=lax.Precision.HIGHEST)
        attended_f = attention_numerator * (total / denominator)[:, None]
        scaled = upstream.astype(jnp.float32) / denominator[:, None]
        coupling = jnp.sum(scaled * attended_f, axis=1)
        scaled_block = scaled.astype(jnp.bfloat16)
        state_grad = jnp.dot(query_random_features.T, scaled_block, preferred_element_type=jnp.float32)
        normalizer_grad = -jnp.dot(query_float.T, coupling, precision=lax.Precision.HIGHEST)
        block_state_gradient = (state_grad * total).astype(jnp.bfloat16)
        query_phi_grad = total * jnp.dot(scaled_block, block_state.T, preferred_element_type=jnp.float32) - coupling[:, None] * normalizer[None, :]
        query_proj_grad = (query_phi_grad * query_float).astype(jnp.bfloat16)
        query_grad = jnp.dot(query_proj_grad, feature_matrix.T, preferred_element_type=jnp.float32) / root_four
        key_phi_grad = jnp.dot(block_value, block_state_gradient.T, preferred_element_type=jnp.float32) / total + normalizer_grad[None, :]
        key_proj_grad = key_phi_grad * key_random_features.astype(jnp.float32)
        key_grad = jnp.dot(key_proj_grad.astype(jnp.bfloat16), feature_matrix.T, preferred_element_type=jnp.float32) / root_four
        key_grad = key_grad - jnp.sum(key_proj_grad, axis=1)[:, None] * key_float / root_two
        value_grad = jnp.dot(key_random_features, block_state_gradient, preferred_element_type=jnp.float32) / total
        return (attended_f.astype(jnp.bfloat16), query_grad.astype(jnp.bfloat16), key_grad.astype(jnp.bfloat16), value_grad.astype(jnp.bfloat16))

    operands = (heads_first(query_vals), spread_scale(query_scale, count).T, heads_first(key_vals), spread_scale(key_scale, count).T, heads_first(value_vals), spread_scale(value_scale, count).T, heads_first(cotangent))
    attended, query_grad, key_grad, value_grad = lax.map(head_pass, operands)
    return (attended.transpose(1, 0, 2).reshape(count, H * DH), query_grad.transpose(1, 0, 2).reshape(count, H * DH), key_grad.transpose(1, 0, 2).reshape(count, H * DH), value_grad.transpose(1, 0, 2).reshape(count, H * DH))
```

```python
import functools

import jax
import jax.numpy as jnp
from jax import lax
from jax.experimental import pallas as pl
from jax.experimental.pallas import tpu as pltpu
from jax.sharding import PartitionSpec as P

F32 = jnp.float32
BF16 = jnp.bfloat16
ANY = pl.BlockSpec(memory_space=pl.ANY)
SMEM = pl.BlockSpec(memory_space=pltpu.SMEM)
VMEM = pl.BlockSpec(memory_space=pltpu.VMEM)
MESH = pl.DeviceIdType.MESH
VMEM_BYTES = 60 << 20
CHUNKS = 4


def dot(a, b, dims=((1,), (0,))):
    return lax.dot_general(a, b, (dims, ((), ())), preferred_element_type=F32)


class Reducer:
    def __init__(self, devices, rows, acc, landing, full, norm, norm_landing, sems):
        self.levels = devices.bit_length() - 1
        self.rows = rows
        self.acc, self.landing, self.full = acc, landing, full
        self.norm, self.norm_landing = norm, norm_landing
        self.send, self.recv, self.nsend, self.nrecv, self.gsend, self.grecv = sems
        self.me = lax.axis_index("seq")
        self.at = {}
        self.pending = {}
        self.sends = []

    def bit(self, chunk, level):
        order = list(range(self.levels))
        if chunk % CHUNKS == CHUNKS - 1 and self.levels > 2:
            order[1], order[2] = order[2], order[1]
        return 1 << order[level]

    def side(self, bit):
        return (self.me // bit) % 2

    def partner(self, bit):
        return self.me + bit - 2 * bit * self.side(bit)

    def greet(self):
        barrier = pltpu.get_barrier_semaphore()
        for level in range(self.levels):
            pl.semaphore_signal(
                barrier, inc=1, device_id={"seq": self.partner(1 << level)}, device_id_type=MESH
            )
        pl.semaphore_wait(barrier, self.levels)

    def offset(self, chunk, level):
        off = 0
        for s in range(level):
            off = off + self.side(self.bit(chunk, s)) * (self.rows >> (s + 1))
        return off

    def span(self, off, size):
        return pl.ds(pl.multiple_of(off, 8), size)

    def copy(self, src, dst, send, recv, bit):
        move = pltpu.make_async_remote_copy(
            src_ref=src, dst_ref=dst, send_sem=send, recv_sem=recv,
            device_id={"seq": self.partner(bit)}, device_id_type=MESH,
        )
        move.start()
        self.sends.append(move)
        return move

    def done(self, chunk):
        return self.at.get(chunk, 0) > 2 * self.levels

    def advance(self, chunk):
        step = self.at.get(chunk, 0)
        if step > 2 * self.levels:
            return
        levels = self.levels
        for move in self.pending.get(chunk, ()):
            move.wait_recv()
        if 1 <= step <= levels:
            last = step - 1
            half = self.rows >> step
            rows = self.span(self.offset(chunk, step), half)
            place = self.rows - (self.rows >> last)
            into = self.full if step == levels else self.acc
            into[chunk, rows, :] = (
                self.acc[chunk, rows, :] + self.landing[chunk, place : place + half, :]
            )
            self.norm[chunk, step] = self.norm[chunk, last] + self.norm_landing[chunk, last]
        if step < levels:
            bit = self.bit(chunk, step)
            half = self.rows >> (step + 1)
            away = self.offset(chunk, step) + (1 - self.side(bit)) * half
            place = self.rows - (self.rows >> step)
            self.pending[chunk] = (
                self.copy(
                    self.acc.at[chunk, self.span(away, half), :],
                    self.landing.at[chunk, place : place + half, :],
                    self.send.at[chunk, step], self.recv.at[chunk, step], bit,
                ),
                self.copy(
                    self.norm.at[chunk, step], self.norm_landing.at[chunk, step],
                    self.nsend.at[chunk, step], self.nrecv.at[chunk, step], bit,
                ),
            )
        elif step < 2 * levels:
            level = 2 * levels - step
            bit = self.bit(chunk, level - 1)
            rows = self.span(self.offset(chunk, level), self.rows >> level)
            self.pending[chunk] = (
                self.copy(
                    self.full.at[chunk, rows, :], self.full.at[chunk, rows, :],
                    self.gsend.at[chunk, level - 1], self.grecv.at[chunk, level - 1], bit,
                ),
            )
        self.at[chunk] = step + 1

    def finish(self):
        while not all(self.done(chunk) for chunk in range(CHUNKS)):
            for chunk in range(CHUNKS):
                self.advance(chunk)
        for move in self.sends:
            move.wait_send()


def reducer_scratch(devices, heads, features, width):
    levels = devices.bit_length() - 1
    rows = heads * features // CHUNKS
    dma = pltpu.SemaphoreType.DMA((CHUNKS, levels))
    return [
        pltpu.VMEM((CHUNKS, rows, width), F32),
        pltpu.VMEM((CHUNKS, rows, width), F32),
        pltpu.VMEM((CHUNKS, rows, width), F32),
        pltpu.VMEM((CHUNKS, levels + 1, heads // CHUNKS, features), F32),
        pltpu.VMEM((CHUNKS, levels, heads // CHUNKS, features), F32),
    ] + [dma] * 6


def key_kernel(
    devices, heads, blocks,
    k_hbm, v_hbm, q_hbm, ks, vs, qs, w,
    state_out, norm_out, kphi_out, qphi_out,
    kbuf, vbuf, qbuf, vb, kphi, qphi,
    acc, landing, full, norm, norm_landing, s0, s1, s2, s3, s4, s5, in_sem, out_sem,
):
    width, features = w.shape
    count = kbuf.shape[0]
    block = count // blocks
    per = heads // CHUNKS
    root_four, root_two = width**0.25, width**0.5
    loads = []
    for group, (src, dst) in enumerate(((k_hbm, kbuf), (v_hbm, vbuf), (q_hbm, qbuf))):
        loads.append([])
        for c in range(CHUNKS):
            cols = slice(c * per * width, (c + 1) * per * width)
            loads[group].append(
                pltpu.make_async_copy(src.at[:, cols], dst.at[:, cols], in_sem.at[group, c])
            )
    for c in range(CHUNKS):
        loads[0][c].start()
        loads[1][c].start()
    for c in range(CHUNKS):
        loads[2][c].start()
    red = Reducer(
        devices, per * features, acc, landing, full, norm, norm_landing, (s0, s1, s2, s3, s4, s5)
    )
    red.greet()
    stores = []

    def key_head(c, i, _):
        h = c * per + i
        cols = pl.ds(pl.multiple_of(h * width, width), width)
        proj = dot(kbuf[:, cols], w[...])
        total = jnp.zeros((1, features), F32)
        for b in range(blocks):
            rows = slice(b * block, (b + 1) * block)
            kf = kbuf[rows, cols].astype(F32) * ks[b, h]
            half_norm = jnp.sum(kf * kf, axis=1, keepdims=True) / (2.0 * root_two)
            phi = jnp.exp(proj[rows] * (ks[b, h] / root_four) - half_norm).astype(BF16)
            kphi[h, rows, :] = phi
            total = total + jnp.sum(phi.astype(F32), axis=0, keepdims=True)
            vb[rows, :] = (vbuf[rows, cols].astype(F32) * vs[b, h]).astype(BF16)
        acc[c, pl.ds(pl.multiple_of(i * features, features), features), :] = dot(
            kphi[h], vb[...], ((0,), (0,))
        )
        norm[c, 0, pl.ds(i, 1), :] = total
        return 0

    def query_head(h, _):
        cols = pl.ds(pl.multiple_of(h * width, width), width)
        proj = dot(qbuf[:, cols], w[...])
        for b in range(blocks):
            rows = slice(b * block, (b + 1) * block)
            qphi[h, rows, :] = jnp.exp(proj[rows] * (qs[b, h] / root_four)).astype(BF16)
        return 0

    for c in range(CHUNKS):
        loads[0][c].wait()
        loads[1][c].wait()
        lax.fori_loop(0, per, functools.partial(key_head, c), 0)
        for before in range(c + 1):
            red.advance(before)
        some = slice(c * per, (c + 1) * per)
        stores.append(pltpu.make_async_copy(kphi.at[some], kphi_out.at[some], out_sem.at[0, c]))
        stores[-1].start()
    for c in range(CHUNKS):
        loads[2][c].wait()
        for part in range(2):
            start = c * per + part * per // 2
            lax.fori_loop(start, start + per // 2, query_head, 0)
            for chunk in range(CHUNKS):
                red.advance(chunk)
        some = slice(c * per, (c + 1) * per)
        stores.append(pltpu.make_async_copy(qphi.at[some], qphi_out.at[some], out_sem.at[1, c]))
        stores[-1].start()
    red.finish()
    for c in range(CHUNKS):
        state_out[c] = full[c]
        norm_out[c] = norm[c, red.levels]
    for store in stores:
        store.wait()


def query_kernel(
    devices, heads,
    qphi_hbm, cot_hbm, state, norm_in, w,
    grad_out, norm_grad_out, att_hbm, qg_hbm,
    qphi, cot, att, qg, scb, stb, coup,
    acc, landing, full, norm, norm_landing, s0, s1, s2, s3, s4, s5, in_sem, out_sem,
):
    width, features = w.shape
    per = heads // CHUNKS
    root_four = width**0.25
    loads, stores = [], []
    for c in range(CHUNKS):
        cols = slice(c * per * width, (c + 1) * per * width)
        some = slice(c * per, (c + 1) * per)
        loads.append((
            pltpu.make_async_copy(qphi_hbm.at[some], qphi.at[some], in_sem.at[0, c]),
            pltpu.make_async_copy(cot_hbm.at[:, cols], cot.at[:, cols], in_sem.at[1, c]),
        ))
        for move in loads[-1]:
            move.start()
    red = Reducer(
        devices, per * features, acc, landing, full, norm, norm_landing, (s0, s1, s2, s3, s4, s5)
    )
    red.greet()

    def forward_head(c, i, _):
        h = c * per + i
        cols = pl.ds(pl.multiple_of(h * width, width), width)
        rows = pl.ds(pl.multiple_of(i * features, features), features)
        n = norm_in[c, pl.ds(i, 1), :]
        total = jnp.sum(n, axis=1, keepdims=True)
        block_state = (state[c, rows, :] / total).astype(BF16)
        stb[c, rows, :] = block_state
        phi = qphi[h].astype(F32)
        numerator = dot(qphi[h], block_state)
        inverse = 1.0 / jnp.sum(phi * n, axis=1, keepdims=True)
        attended = numerator * (total * inverse)
        att[:, cols] = attended.astype(BF16)
        scaled = cot[:, cols].astype(F32) * inverse
        coupling = jnp.sum(scaled * attended, axis=1, keepdims=True)
        coup[h] = coupling
        scb[:, cols] = scaled.astype(BF16)
        acc[c, rows, :] = dot(qphi[h], scb[:, cols], ((0,), (0,)))
        norm[c, 0, pl.ds(i, 1), :] = -jnp.sum(coupling * phi, axis=0, keepdims=True)
        return 0

    def grad_head(c, i, _):
        h = c * per + i
        cols = pl.ds(pl.multiple_of(h * width, width), width)
        rows = pl.ds(pl.multiple_of(i * features, features), features)
        n = norm_in[c, pl.ds(i, 1), :]
        total = jnp.sum(n, axis=1, keepdims=True)
        phi_grad = total * dot(scb[:, cols], stb[c, rows, :], ((1,), (1,))) - coup[h] * n
        proj_grad = (phi_grad * qphi[h].astype(F32)).astype(BF16)
        qg[:, cols] = (dot(proj_grad, w[...], ((1,), (1,))) / root_four).astype(BF16)
        return 0

    for c in range(CHUNKS):
        for move in loads[c]:
            move.wait()
        lax.fori_loop(0, per, functools.partial(forward_head, c), 0)
        for before in range(c + 1):
            red.advance(before)
        cols = slice(c * per * width, (c + 1) * per * width)
        stores.append(pltpu.make_async_copy(att.at[:, cols], att_hbm.at[:, cols], out_sem.at[0, c]))
        stores[-1].start()
    for c in range(CHUNKS):
        for part in range(2):
            start = part * per // 2
            lax.fori_loop(start, start + per // 2, functools.partial(grad_head, c), 0)
            for chunk in range(CHUNKS):
                red.advance(chunk)
        cols = slice(c * per * width, (c + 1) * per * width)
        stores.append(pltpu.make_async_copy(qg.at[:, cols], qg_hbm.at[:, cols], out_sem.at[1, c]))
        stores[-1].start()
    red.finish()
    for c in range(CHUNKS):
        grad_out[c] = full[c]
        norm_grad_out[c] = norm[c, red.levels]
    for store in stores:
        store.wait()


def value_kernel(blocks, k, v, kphi, grad, norm_in, norm_grad, ks, vs, w, kg, vg, vb):
    h = pl.program_id(0)
    width = w.shape[0]
    block = k.shape[0] // blocks
    root_four, root_two = width**0.25, width**0.5
    total = jnp.sum(norm_in[pl.ds(h, 1), :], axis=1, keepdims=True)
    inverse = 1.0 / total
    block_grad = (grad[0] * total).astype(BF16)
    for b in range(blocks):
        rows = slice(b * block, (b + 1) * block)
        vb[rows, :] = (v[rows, :].astype(F32) * vs[b, h]).astype(BF16)
    proj_grad = (
        dot(vb[...], block_grad, ((1,), (1,))) * inverse + norm_grad[pl.ds(h, 1), :]
    ) * kphi[0].astype(F32)
    sums = jnp.sum(proj_grad, axis=1, keepdims=True) / root_two
    out = dot(proj_grad.astype(BF16), w[...], ((1,), (1,))) / root_four
    for b in range(blocks):
        rows = slice(b * block, (b + 1) * block)
        kf = k[rows, :].astype(F32) * ks[b, h]
        kg[rows, :] = (out[rows] - sums[rows] * kf).astype(BF16)
    vg[...] = (dot(kphi[0], block_grad) * inverse).astype(BF16)


def per_device(
    devices,
    query_vals, query_scale, key_vals, key_scale, value_vals, value_scale, feature_matrix, cotangent,
):
    count, flat = query_vals.shape
    blocks, heads = query_scale.shape
    width, features = feature_matrix.shape
    per = heads // CHUNKS
    shape = jax.ShapeDtypeStruct
    phi_shape = shape((heads, count, features), BF16)
    state_shape = shape((CHUNKS, per * features, width), F32)
    norm_shape = shape((CHUNKS, per, features), F32)
    flat_shape = shape((count, flat), BF16)
    flat_scratch = pltpu.VMEM((count, flat), BF16)
    phi_scratch = pltpu.VMEM((heads, count, features), BF16)
    shared = reducer_scratch(devices, heads, features, width)

    def params(number):
        return pltpu.CompilerParams(
            collective_id=number, has_side_effects=True, vmem_limit_bytes=VMEM_BYTES
        )

    state, normalizer, kphi, qphi = pl.pallas_call(
        functools.partial(key_kernel, devices, heads, blocks),
        out_shape=(state_shape, norm_shape, phi_shape, phi_shape),
        in_specs=[ANY, ANY, ANY, SMEM, SMEM, SMEM, VMEM],
        out_specs=(VMEM, VMEM, ANY, ANY),
        scratch_shapes=[
            flat_scratch, flat_scratch, flat_scratch, pltpu.VMEM((count, width), BF16),
            phi_scratch, phi_scratch, *shared,
            pltpu.SemaphoreType.DMA((3, CHUNKS)), pltpu.SemaphoreType.DMA((2, CHUNKS)),
        ],
        compiler_params=params(0),
        name="key_state",
    )(key_vals, value_vals, query_vals, key_scale, value_scale, query_scale, feature_matrix)

    state_grad, norm_grad, attended, query_grad = pl.pallas_call(
        functools.partial(query_kernel, devices, heads),
        out_shape=(state_shape, norm_shape, flat_shape, flat_shape),
        in_specs=[ANY, ANY, VMEM, VMEM, VMEM],
        out_specs=(VMEM, VMEM, ANY, ANY),
        scratch_shapes=[
            phi_scratch, flat_scratch, flat_scratch, flat_scratch, flat_scratch,
            pltpu.VMEM((CHUNKS, per * features, width), BF16),
            pltpu.VMEM((heads, count, 1), F32), *shared,
            pltpu.SemaphoreType.DMA((2, CHUNKS)), pltpu.SemaphoreType.DMA((2, CHUNKS)),
        ],
        compiler_params=params(1),
        name="query_grad",
    )(qphi, cotangent, state, normalizer, feature_matrix)

    column = pl.BlockSpec((count, width), lambda h: (0, h))
    whole = pl.BlockSpec((heads, features), lambda h: (0, 0))
    key_grad, value_grad = pl.pallas_call(
        functools.partial(value_kernel, blocks),
        grid=(heads,),
        out_shape=(flat_shape, flat_shape),
        in_specs=[
            column, column,
            pl.BlockSpec((1, count, features), lambda h: (h, 0, 0)),
            pl.BlockSpec((1, features, width), lambda h: (h, 0, 0)),
            whole, whole, SMEM, SMEM,
            pl.BlockSpec((width, features), lambda h: (0, 0)),
        ],
        out_specs=(column, column),
        scratch_shapes=[pltpu.VMEM((count, width), BF16)],
        compiler_params=pltpu.CompilerParams(vmem_limit_bytes=VMEM_BYTES),
        name="key_grad",
    )(
        key_vals, value_vals, kphi, state_grad.reshape(heads, features, width),
        normalizer.reshape(heads, features), norm_grad.reshape(heads, features),
        key_scale, value_scale, feature_matrix,
    )
    return attended, query_grad, key_grad, value_grad


def solution(mesh):
    rows = P(("groups", "seq"), None)
    return jax.shard_map(
        functools.partial(per_device, mesh.shape["seq"]),
        mesh=mesh,
        in_specs=(rows, rows, rows, rows, rows, rows, P(), rows),
        out_specs=(rows, rows, rows, rows),
        check_vma=False,
    )
```

```python
import functools

import jax
import jax.numpy as jnp
from jax import lax
from jax.experimental import pallas as pl
from jax.experimental.pallas import tpu as pltpu
from jax.sharding import PartitionSpec as P

F32 = jnp.float32
BF16 = jnp.bfloat16
ANY = pl.BlockSpec(memory_space=pl.ANY)
SMEM = pl.BlockSpec(memory_space=pltpu.SMEM)
VMEM = pl.BlockSpec(memory_space=pltpu.VMEM)
MESH = pl.DeviceIdType.MESH
VMEM_BYTES = 60 << 20
CHUNKS = 4
PAIR = 2
STEP_HEADS = 2


def dot(a, b, dims=((1,), (0,))):
    return lax.dot_general(a, b, (dims, ((), ())), preferred_element_type=F32)


def each_head(start, stop, body):
    def step(j, _):
        for k in range(PAIR):
            body(start + j * PAIR + k)
        return 0

    lax.fori_loop(0, (stop - start) // PAIR, step, 0)


class Reducer:
    def __init__(self, devices, rows, acc, landing, full, norm, norm_landing, sems):
        self.levels = devices.bit_length() - 1
        self.rows = rows
        self.acc, self.landing, self.full = acc, landing, full
        self.norm, self.norm_landing = norm, norm_landing
        self.send, self.recv, self.nsend, self.nrecv, self.gsend, self.grecv = sems
        self.me = lax.axis_index("seq")
        self.at = {}
        self.pending = {}
        self.sends = []

    def bit(self, chunk, level):
        order = list(range(self.levels))
        if chunk % 2 and self.levels > 2:
            order[1], order[2] = order[2], order[1]
        return 1 << order[level]

    def side(self, bit):
        return (self.me // bit) % 2

    def partner(self, bit):
        return self.me + bit - 2 * bit * self.side(bit)

    def greet(self):
        barrier = pltpu.get_barrier_semaphore()
        for level in range(self.levels):
            pl.semaphore_signal(
                barrier, inc=1, device_id={"seq": self.partner(1 << level)}, device_id_type=MESH
            )
        pl.semaphore_wait(barrier, self.levels)

    def offset(self, chunk, level):
        off = 0
        for s in range(level):
            off = off + self.side(self.bit(chunk, s)) * (self.rows >> (s + 1))
        return off

    def span(self, off, size):
        return pl.ds(pl.multiple_of(off, 8), size)

    def copy(self, src, dst, send, recv, bit):
        move = pltpu.make_async_remote_copy(
            src_ref=src, dst_ref=dst, send_sem=send, recv_sem=recv,
            device_id={"seq": self.partner(bit)}, device_id_type=MESH,
        )
        move.start()
        self.sends.append(move)
        return move

    def done(self, chunk):
        return self.at.get(chunk, 0) > 2 * self.levels

    def advance(self, chunk):
        step = self.at.get(chunk, 0)
        if step > 2 * self.levels:
            return
        levels = self.levels
        for move in self.pending.get(chunk, ()):
            move.wait_recv()
        if 1 <= step <= levels:
            last = step - 1
            half = self.rows >> step
            rows = self.span(self.offset(chunk, step), half)
            place = self.rows - (self.rows >> last)
            into = self.full if step == levels else self.acc
            into[chunk, rows, :] = (
                self.acc[chunk, rows, :] + self.landing[chunk, place : place + half, :]
            )
            self.norm[chunk, step] = self.norm[chunk, last] + self.norm_landing[chunk, last]
        if step < levels:
            bit = self.bit(chunk, step)
            half = self.rows >> (step + 1)
            away = self.offset(chunk, step) + (1 - self.side(bit)) * half
            place = self.rows - (self.rows >> step)
            self.pending[chunk] = (
                self.copy(
                    self.acc.at[chunk, self.span(away, half), :],
                    self.landing.at[chunk, place : place + half, :],
                    self.send.at[chunk, step], self.recv.at[chunk, step], bit,
                ),
                self.copy(
                    self.norm.at[chunk, step], self.norm_landing.at[chunk, step],
                    self.nsend.at[chunk, step], self.nrecv.at[chunk, step], bit,
                ),
            )
        elif step < 2 * levels:
            level = 2 * levels - step
            bit = self.bit(chunk, level - 1)
            rows = self.span(self.offset(chunk, level), self.rows >> level)
            self.pending[chunk] = (
                self.copy(
                    self.full.at[chunk, rows, :], self.full.at[chunk, rows, :],
                    self.gsend.at[chunk, level - 1], self.grecv.at[chunk, level - 1], bit,
                ),
            )
        self.at[chunk] = step + 1

    def finish(self):
        while not all(self.done(chunk) for chunk in range(CHUNKS)):
            for chunk in range(CHUNKS):
                self.advance(chunk)
        for move in self.sends:
            move.wait_send()


def reducer_scratch(devices, heads, features, width):
    levels = devices.bit_length() - 1
    rows = heads * features // CHUNKS
    dma = pltpu.SemaphoreType.DMA((CHUNKS, levels))
    return [
        pltpu.VMEM((CHUNKS, rows, width), F32),
        pltpu.VMEM((CHUNKS, rows, width), F32),
        pltpu.VMEM((CHUNKS, rows, width), F32),
        pltpu.VMEM((CHUNKS, levels + 1, heads // CHUNKS, features), F32),
        pltpu.VMEM((CHUNKS, levels, heads // CHUNKS, features), F32),
    ] + [dma] * 6


def main_kernel(
    devices, heads, blocks,
    k_hbm, v_hbm, q_hbm, cot_hbm, ks, vs, qs, w,
    norm_out, grad_out, norm_grad_out, kphi_out, att_hbm, qg_hbm,
    kbuf, vbuf, qbuf, vb, kphi, qphi, cot, scb, stb, coup, in_sem, out_sem, *shared,
):
    width, features = w.shape
    count = kbuf.shape[0]
    block = count // blocks
    per = heads // CHUNKS
    root_four, root_two = width**0.25, width**0.5
    att, qg = kbuf, vbuf
    spans = [slice(c * per * width, (c + 1) * per * width) for c in range(CHUNKS)]
    loads = []
    for group, (src, dst) in enumerate(
        ((k_hbm, kbuf), (v_hbm, vbuf), (q_hbm, qbuf), (cot_hbm, cot))
    ):
        loads.append([
            pltpu.make_async_copy(src.at[:, cols], dst.at[:, cols], in_sem.at[group, c])
            for c, cols in enumerate(spans)
        ])
    for c in range(CHUNKS):
        loads[0][c].start()
        loads[1][c].start()
    for c in range(CHUNKS):
        loads[2][c].start()
    for c in range(CHUNKS):
        loads[3][c].start()
    half = len(shared) // 2
    first = Reducer(devices, per * features, *shared[:5], shared[5:half])
    second = Reducer(devices, per * features, *shared[half : half + 5], shared[half + 5 :])
    first.greet()
    stores = []

    def key_head(c, i):
        h = c * per + i
        cols = pl.ds(pl.multiple_of(h * width, width), width)
        proj = dot(kbuf[:, cols], w[...])
        total = jnp.zeros((1, features), F32)
        for b in range(blocks):
            rows = slice(b * block, (b + 1) * block)
            kf = kbuf[rows, cols].astype(F32) * ks[b, h]
            half_norm = jnp.sum(kf * kf, axis=1, keepdims=True) / (2.0 * root_two)
            phi = jnp.exp(proj[rows] * (ks[b, h] / root_four) - half_norm).astype(BF16)
            kphi[h, rows, :] = phi
            total = total + jnp.sum(phi.astype(F32), axis=0, keepdims=True)
            vb[i % PAIR, rows, :] = (vbuf[rows, cols].astype(F32) * vs[b, h]).astype(BF16)
        first.acc[c, pl.ds(pl.multiple_of(i * features, features), features), :] = dot(
            kphi[h], vb[i % PAIR], ((0,), (0,))
        )
        first.norm[c, 0, pl.ds(i, 1), :] = total

    def query_head(h):
        cols = pl.ds(pl.multiple_of(h * width, width), width)
        proj = dot(qbuf[:, cols], w[...])
        for b in range(blocks):
            rows = slice(b * block, (b + 1) * block)
            qphi[h, rows, :] = jnp.exp(proj[rows] * (qs[b, h] / root_four)).astype(BF16)

    def forward_head(c, i):
        h = c * per + i
        cols = pl.ds(pl.multiple_of(h * width, width), width)
        rows = pl.ds(pl.multiple_of(i * features, features), features)
        n = first.norm[c, first.levels, pl.ds(i, 1), :]
        total = jnp.sum(n, axis=1, keepdims=True)
        block_state = (first.full[c, rows, :] / total).astype(BF16)
        stb[c, rows, :] = block_state
        phi = qphi[h].astype(F32)
        numerator = dot(qphi[h], block_state)
        inverse = 1.0 / jnp.sum(phi * n, axis=1, keepdims=True)
        attended = numerator * (total * inverse)
        att[:, cols] = attended.astype(BF16)
        scaled = cot[:, cols].astype(F32) * inverse
        coupling = jnp.sum(scaled * attended, axis=1, keepdims=True)
        coup[h] = coupling
        scb[:, cols] = scaled.astype(BF16)
        second.acc[c, rows, :] = dot(qphi[h], scb[:, cols], ((0,), (0,)))
        second.norm[c, 0, pl.ds(i, 1), :] = -jnp.sum(coupling * phi, axis=0, keepdims=True)

    def grad_head(c, i):
        h = c * per + i
        cols = pl.ds(pl.multiple_of(h * width, width), width)
        rows = pl.ds(pl.multiple_of(i * features, features), features)
        n = first.norm[c, first.levels, pl.ds(i, 1), :]
        total = jnp.sum(n, axis=1, keepdims=True)
        phi_grad = total * dot(scb[:, cols], stb[c, rows, :], ((1,), (1,))) - coup[h] * n
        proj_grad = (phi_grad * qphi[h].astype(F32)).astype(BF16)
        qg[:, cols] = (dot(proj_grad, w[...], ((1,), (1,))) / root_four).astype(BF16)

    def store(src, dst, group, c):
        stores.append(pltpu.make_async_copy(src, dst, out_sem.at[group, c]))
        stores[-1].start()

    forwarded = set()
    fillers = []
    for c in range(CHUNKS):
        for part in range(2):
            fillers.append((True, c, part))

    def fill():
        if not fillers:
            return
        early, c, part = fillers[0]
        if not early and c not in forwarded:
            return
        fillers.pop(0)
        start = part * per // 2
        if early:
            if part == 0:
                loads[2][c].wait()
            each_head(c * per + start, c * per + start + per // 2, query_head)
            return
        each_head(start, start + per // 2, functools.partial(grad_head, c))
        if part == 1:
            store(qg.at[:, spans[c]], qg_hbm.at[:, spans[c]], 2, c)

    def move(c):
        if not first.done(c):
            first.advance(c)
        elif c in forwarded:
            second.advance(c)
        elif not any(early and at == c for early, at, _ in fillers):
            loads[3][c].wait()
            each_head(0, per, functools.partial(forward_head, c))
            second.advance(c)
            store(att.at[:, spans[c]], att_hbm.at[:, spans[c]], 1, c)
            forwarded.add(c)
            fillers.extend((False, c, part) for part in range(2))

    for c in range(CHUNKS):
        loads[0][c].wait()
        loads[1][c].wait()
        each_head(0, per, functools.partial(key_head, c))
        for before in range(c + 1):
            first.advance(before)
        some = slice(c * per, (c + 1) * per)
        store(kphi.at[some], kphi_out.at[some], 0, c)
    while fillers or not all(second.done(c) for c in range(CHUNKS)):
        fill()
        for c in range(CHUNKS):
            move(c)
    first.finish()
    second.finish()
    for c in range(CHUNKS):
        norm_out[c] = first.norm[c, first.levels]
        grad_out[c] = second.full[c]
        norm_grad_out[c] = second.norm[c, second.levels]
    for each in stores:
        each.wait()


def value_kernel(blocks, k, v, kphi, grad, norm_in, norm_grad, ks, vs, w, kg, vg, vb):
    width = w.shape[0]
    per = norm_in.shape[1]
    block = k.shape[0] // blocks
    root_four, root_two = width**0.25, width**0.5
    for i in range(STEP_HEADS):
        h = pl.program_id(0) * STEP_HEADS + i
        cols = slice(i * width, (i + 1) * width)
        total = jnp.sum(norm_in[h // per, pl.ds(h % per, 1), :], axis=1, keepdims=True)
        inverse = 1.0 / total
        block_grad = (grad[i] * total).astype(BF16)
        for b in range(blocks):
            rows = slice(b * block, (b + 1) * block)
            vb[i, rows, :] = (v[rows, cols].astype(F32) * vs[b, h]).astype(BF16)
        proj_grad = (
            dot(vb[i], block_grad, ((1,), (1,))) * inverse
            + norm_grad[h // per, pl.ds(h % per, 1), :]
        ) * kphi[i].astype(F32)
        sums = jnp.sum(proj_grad, axis=1, keepdims=True) / root_two
        out = dot(proj_grad.astype(BF16), w[...], ((1,), (1,))) / root_four
        for b in range(blocks):
            rows = slice(b * block, (b + 1) * block)
            kf = k[rows, cols].astype(F32) * ks[b, h]
            kg[rows, cols] = (out[rows] - sums[rows] * kf).astype(BF16)
        vg[:, cols] = (dot(kphi[i], block_grad) * inverse).astype(BF16)


def per_device(
    devices,
    query_vals, query_scale, key_vals, key_scale, value_vals, value_scale, feature_matrix, cotangent,
):
    count, flat = query_vals.shape
    blocks, heads = query_scale.shape
    width, features = feature_matrix.shape
    per = heads // CHUNKS
    shape = jax.ShapeDtypeStruct
    phi_shape = shape((heads, count, features), BF16)
    state_shape = shape((CHUNKS, per * features, width), F32)
    norm_shape = shape((CHUNKS, per, features), F32)
    flat_shape = shape((count, flat), BF16)
    flat_scratch = pltpu.VMEM((count, flat), BF16)
    phi_scratch = pltpu.VMEM((heads, count, features), BF16)
    shared = reducer_scratch(devices, heads, features, width)

    normalizer, state_grad, norm_grad, kphi, attended, query_grad = pl.pallas_call(
        functools.partial(main_kernel, devices, heads, blocks),
        out_shape=(norm_shape, state_shape, norm_shape, phi_shape, flat_shape, flat_shape),
        in_specs=[ANY, ANY, ANY, ANY, SMEM, SMEM, SMEM, VMEM],
        out_specs=(VMEM, VMEM, VMEM, ANY, ANY, ANY),
        scratch_shapes=[
            flat_scratch, flat_scratch, flat_scratch, pltpu.VMEM((PAIR, count, width), BF16),
            phi_scratch, phi_scratch, flat_scratch, flat_scratch,
            pltpu.VMEM((CHUNKS, per * features, width), BF16),
            pltpu.VMEM((heads, count, 1), F32),
            pltpu.SemaphoreType.DMA((4, CHUNKS)), pltpu.SemaphoreType.DMA((3, CHUNKS)),
            *shared, *shared,
        ],
        compiler_params=pltpu.CompilerParams(
            collective_id=0, has_side_effects=True, vmem_limit_bytes=VMEM_BYTES
        ),
        name="attention",
    )(
        key_vals, value_vals, query_vals, cotangent, key_scale, value_scale, query_scale,
        feature_matrix,
    )

    column = pl.BlockSpec((count, STEP_HEADS * width), lambda h: (0, h))
    whole = pl.BlockSpec((CHUNKS, per, features), lambda h: (0, 0, 0))
    key_grad, value_grad = pl.pallas_call(
        functools.partial(value_kernel, blocks),
        grid=(heads // STEP_HEADS,),
        out_shape=(flat_shape, flat_shape),
        in_specs=[
            column, column,
            pl.BlockSpec((STEP_HEADS, count, features), lambda h: (h, 0, 0)),
            pl.BlockSpec((STEP_HEADS, features, width), lambda h: (h, 0, 0)),
            whole, whole, SMEM, SMEM,
            pl.BlockSpec((width, features), lambda h: (0, 0)),
        ],
        out_specs=(column, column),
        scratch_shapes=[pltpu.VMEM((STEP_HEADS, count, width), BF16)],
        compiler_params=pltpu.CompilerParams(vmem_limit_bytes=VMEM_BYTES),
        name="key_grad",
    )(
        key_vals, value_vals, kphi, state_grad.reshape(heads, features, width),
        normalizer, norm_grad,
        key_scale, value_scale, feature_matrix,
    )
    return attended, query_grad, key_grad, value_grad


def solution(mesh):
    rows = P(("groups", "seq"), None)
    return jax.shard_map(
        functools.partial(per_device, mesh.shape["seq"]),
        mesh=mesh,
        in_specs=(rows, rows, rows, rows, rows, rows, P(), rows),
        out_specs=(rows, rows, rows, rows),
        check_vma=False,
    )
```
